32 devices in a mesh: groups: 2 (over y), rows: 4 (over z), cols: 4 (over x, core).
Axes of the slice: x: 2, y: 2, z: 4, core: 2. Of those that a mesh axis runs over, the one named last changes fastest.
Arguments:
- queries: bfloat16 [4096, 1024], P(('groups', 'rows', 'cols')), parts along dimension 0, may hold values from -4.25 to 4.25
- keys: bfloat16 [4096, 128], P(('groups', 'rows', 'cols')), parts along dimension 0, may hold values from -4.25 to 4.25
- values: bfloat16 [4096, 128], P(('groups', 'rows', 'cols')), parts along dimension 0, may hold values from -6 to 6
- positions: int32 [4096], P(('groups', 'rows', 'cols')), parts along dimension 0, may hold values from 0 to 2047, as said below
Outputs:
- attended: bfloat16 [4096, 1024], P(('groups', 'rows', 'cols')), parts along dimension 0
The draws below stay inside these ranges and needn't reach their ends.
There are 2 independent parts, one for each index of `groups`. The reference program is written for one: setup_inputs(seed, part) draws one part's arguments, and reference() takes and returns one part's arrays. A program takes and returns all parts, laid end to end along the dimension named above; each array names one. Nothing has to cross between parts.
Inputs may be any that keep to these rules, and one draw needn't show every extreme that they name: `positions`: a permutation of 0 to 2047.
All inputs are finite; a program needn't handle non-finite values.
Results may differ from the reference program's by a relative error of at most 0.015.
Values may be sent and summed in bfloat16 or wider, within the bound.
No kernel may reach another device: no remote copies, remote signals or barrier semaphores. Data moves between devices by JAX's collectives and lax.ppermute only.
A program may use at most 64 MiB of HBM per device.

```python
import math
import jax
import jax.numpy as jnp
from jax import lax

HEADS = 8
HEAD_DIM = 128
TOKENS = 2048


def shared_order(key):
    order = jax.random.permutation(jax.random.fold_in(key, 11), TOKENS).astype(jnp.int32)
    return order


def draw_positions(key, part):
    return shared_order(key)


def draw_keys(key, part):
    base = jnp.clip(jax.random.normal(jax.random.fold_in(key, 12), (TOKENS, HEAD_DIM), jnp.float32), -4.0, 4.0)
    return base.astype(jnp.bfloat16)


def draw_queries(key, part):
    base = jnp.clip(jax.random.normal(jax.random.fold_in(key, 14), (TOKENS, HEADS * HEAD_DIM), jnp.float32), -4.0, 4.0)
    return base.astype(jnp.bfloat16)


def block_scale(key, extent, shards, smallest, high):
    gain = 1.0
    for dim, blocks in shards:
        draws = jax.random.uniform(jax.random.fold_in(jax.random.fold_in(key, 6), dim), (blocks,), jnp.float32, smallest / len(shards), high / len(shards))
        gain = gain * jnp.repeat(jnp.exp(draws), extent[dim] // blocks).reshape((-1,) + (1,) * (len(extent) - 1 - dim))
    return gain


def scatter_about(stream_key, dims, width, reach, pieces=(), held_as=jnp.bfloat16):
    drawn = width * jax.random.normal(stream_key, dims, jnp.float32)
    if pieces:
        drawn = drawn * block_scale(stream_key, dims, pieces, -0.22, 0.18)
    return jnp.clip(drawn, -reach, reach).astype(held_as)


def setup_inputs(seed: int = 0, part: int = 0) -> dict:
    key_of = jax.random.split(jax.random.key(seed), 5)
    part_splits = jax.random.split(jax.random.fold_in(key_of[4], part), 5)
    return {
        "queries": draw_queries(jax.random.fold_in(jax.random.fold_in(key_of[4], part), 71), part),
        "keys": draw_keys(jax.random.fold_in(jax.random.fold_in(key_of[4], part), 71), part),
        "values": scatter_about(part_splits[2], (TOKENS, HEAD_DIM), 1.0, 6.0, ((0, 16),)),
        "positions": draw_positions(jax.random.fold_in(jax.random.fold_in(key_of[4], part), 71), part),
    }


def reference(queries, keys, values, positions):
    total = queries.shape[0]
    block = math.gcd(total, 256)
    scale = HEAD_DIM ** -0.5
    query_heads = queries.reshape(total // block, block, HEADS, HEAD_DIM)
    query_pos = positions.reshape(total // block, block)
    keys_wide = keys.astype(jnp.float32)
    values_wide = values.astype(jnp.float32)

    def one_block(item):
        query_tile, pos_tile = item
        scores = jnp.einsum("qhd,kd->qhk", query_tile.astype(jnp.float32), keys_wide) * scale
        visible = positions[None, None, :] <= pos_tile[:, None, None]
        row_max = jnp.max(jnp.where(visible, scores, -1e30), axis=2, keepdims=True)
        weights = jnp.where(visible, jnp.exp(scores - row_max), 0.0).astype(jnp.bfloat16)
        wide = weights.astype(jnp.float32)
        denominators = jnp.sum(wide, axis=2)
        numerators = jnp.einsum("qhk,kd->qhd", wide, values_wide)
        result = (numerators / denominators[:, :, None]).astype(jnp.bfloat16)
        return result.reshape(block, HEADS * HEAD_DIM)

    return lax.map(one_block, (query_heads, query_pos)).reshape(total, HEADS * HEAD_DIM)
```

```python
import functools
import math

import jax
import jax.numpy as jnp
from jax import lax
from jax.experimental import pallas as pl
from jax.experimental.pallas import tpu as pltpu
from jax.sharding import PartitionSpec as P

HEADS = 8
HEAD_DIM = 128
LANES = 128
POS_ROWS = 16
HIGH = 128

den_low = 1e-18
den_high = 1e37
neg_fill = -1e30


def pack(keys, values, positions):
    rows = keys.shape[0]
    high = (positions // HIGH).astype(keys.dtype).reshape(rows // LANES, LANES)
    low = (positions % HIGH).astype(keys.dtype).reshape(rows // LANES, LANES)
    pos = jnp.concatenate([high, low], axis=1)
    pos = jnp.pad(pos, ((0, POS_ROWS - rows // LANES), (0, 0)))
    return jnp.concatenate([jnp.concatenate([keys, values], axis=1), pos], axis=0)[None]


def swap(x, axis, size, bit, name):
    with jax.named_scope(name):
        return lax.ppermute(x, axis, [(i, i ^ bit) for i in range(size)])


def gather(own, rows, cols):
    bit = rows // 2
    while bit >= 4:
        own = jnp.concatenate([own, swap(own, "rows", rows, bit, "wide")], axis=0)
        bit //= 2
    z2 = swap(own, "rows", rows, 2, "z2")
    z1 = swap(own, "rows", rows, 1, "z1")
    xo = swap(own, "cols", cols, 2, "xo")
    z3 = swap(z2, "rows", rows, 1, "z3")
    xz2 = swap(z2, "cols", cols, 2, "xz2")
    xz1 = swap(z1, "cols", cols, 2, "xz1")
    xz3 = swap(z3, "cols", cols, 2, "xz3")
    near = [own, xo, z1, z2, xz2, z3, xz1, xz3]
    far = [swap(b, "cols", cols, 1, "c%d" % i) for i, b in enumerate(near)]
    return [b for pair in zip(near, far) for b in pair]


def key_positions(ref, i, j):
    rows = ref.shape[1] - POS_ROWS
    pair = ref[i, rows : rows + POS_ROWS, :].astype(jnp.float32)[j : j + 1]
    return pair[:, :LANES] * HIGH + pair[:, LANES:]


def attend_kernel(n, count, q_ref, pos_ref, *refs):
    pieces = refs[:count]
    o_ref, qs, acc_ref = refs[count:]
    tokens = q_ref.shape[0]
    block = pieces[0].shape[1] - POS_ROWS
    scale = HEAD_DIM ** (-0.5)
    pre = scale * math.log2(math.e)
    for h in range(HEADS):
        qs[h * tokens : (h + 1) * tokens, :] = q_ref[:, h * HEAD_DIM : (h + 1) * HEAD_DIM]
    query_pos = jnp.transpose(
        jnp.broadcast_to(pos_ref[...].astype(jnp.float32), (LANES, tokens))
    )
    ones = jnp.ones((block, HEAD_DIM), jnp.bfloat16)

    def visible(ref, i):
        return jnp.concatenate(
            [key_positions(ref, i, j) <= query_pos for j in range(block // LANES)], axis=1
        )

    def keys_of(ref, i):
        return ref[i, :block, :HEAD_DIM]

    def values_of(ref, i):
        return jnp.concatenate([ref[i, :block, HEAD_DIM:], ones], axis=1)

    stack = 4 if HEADS % 4 == 0 else 1
    span = stack * tokens

    def fast(i, first):
        for r in range(HEADS // stack):
            q = qs[r * span : (r + 1) * span, :]
            total = None if first else acc_ref[r * span : (r + 1) * span, :]
            for j in range(0, count, 2):
                group = pieces[j : j + 2]
                scores = lax.dot_general(
                    q,
                    jnp.concatenate([keys_of(g, i) for g in group], axis=0),
                    (((1,), (1,)), ((), ())),
                    preferred_element_type=jnp.float32,
                )
                mask = jnp.concatenate([visible(g, i) for g in group], axis=1)
                mask = jnp.concatenate([mask] * stack, axis=0)
                weights = jnp.where(mask, jnp.exp2(scores * pre), 0.0).astype(jnp.bfloat16)
                part = jnp.dot(
                    weights,
                    jnp.concatenate([values_of(g, i) for g in group], axis=0),
                    preferred_element_type=jnp.float32,
                )
                total = part if total is None else total + part
            acc_ref[r * span : (r + 1) * span, :] = total

    fast(0, True)
    if n > 1:
        lax.fori_loop(1, n, lambda i, c: (fast(i, False), c)[1], 0)

    def store():
        for h in range(HEADS):
            part = acc_ref[h * tokens : (h + 1) * tokens, :]
            o_ref[:, h * HEAD_DIM : (h + 1) * HEAD_DIM] = (
                part[:, :HEAD_DIM] / part[:, HEAD_DIM:]
            ).astype(o_ref.dtype)

    store()
    den = acc_ref[:, HEAD_DIM:]
    good = (den >= den_low) & (den <= den_high)
    worst = jnp.min(jnp.where(good, 1.0, 0.0))

    @pl.when(worst < 0.5)
    def _():
        def one_head(h, carry):
            at = pl.ds(pl.multiple_of(h * tokens, tokens), tokens)
            q = qs[at, :]

            def scores_of(ref, i):
                s = lax.dot_general(
                    q, keys_of(ref, i), (((1,), (1,)), ((), ())),
                    preferred_element_type=jnp.float32,
                )
                return s * scale

            def top_of(i, top):
                for ref in pieces:
                    s = jnp.where(visible(ref, i), scores_of(ref, i), neg_fill)
                    top = jnp.maximum(top, jnp.max(s, axis=1, keepdims=True))
                return top

            top = lax.fori_loop(0, n, top_of, jnp.full((tokens, 1), neg_fill, jnp.float32))

            def add(i, total):
                for ref in pieces:
                    w = jnp.where(visible(ref, i), jnp.exp(scores_of(ref, i) - top), 0.0)
                    total = total + jnp.dot(
                        w.astype(jnp.bfloat16), values_of(ref, i),
                        preferred_element_type=jnp.float32,
                    )
                return total

            acc_ref[at, :] = lax.fori_loop(
                0, n, add, jnp.zeros((tokens, 2 * HEAD_DIM), jnp.float32)
            )
            return carry

        lax.fori_loop(0, HEADS, one_head, 0)
        store()


def attend(queries, positions, pieces):
    tokens = queries.shape[0]
    n = pieces[0].shape[0]
    count = len(pieces)
    block = pieces[0].shape[1] - POS_ROWS
    work = tokens * HEADS * n * count * block * HEAD_DIM
    with jax.named_scope("attend"):
        return pl.pallas_call(
            functools.partial(attend_kernel, n, count),
            out_shape=jax.ShapeDtypeStruct(queries.shape, jnp.bfloat16),
            in_specs=[pl.BlockSpec(memory_space=pltpu.VMEM)] * (2 + count),
            out_specs=pl.BlockSpec(memory_space=pltpu.VMEM),
            scratch_shapes=[
                pltpu.VMEM((HEADS * tokens, HEAD_DIM), jnp.bfloat16),
                pltpu.VMEM((HEADS * tokens, 2 * HEAD_DIM), jnp.float32),
            ],
            cost_estimate=pl.CostEstimate(
                flops=4 * work, bytes_accessed=2 * queries.size * 2, transcendentals=0
            ),
            name="attend",
        )(queries, positions.reshape(1, tokens), *pieces)


def solution(mesh):
    rows, cols = mesh.shape["rows"], mesh.shape["cols"]

    def shards(queries, keys, values, positions):
        pieces = gather(pack(keys, values, positions), rows, cols)
        return attend(queries, positions, pieces)

    return jax.shard_map(
        shards,
        mesh=mesh,
        in_specs=(
            P(("groups", "rows", "cols"), None),
            P(("groups", "rows", "cols"), None),
            P(("groups", "rows", "cols"), None),
            P(("groups", "rows", "cols")),
        ),
        out_specs=P(("groups", "rows", "cols"), None),
        check_vma=False,
    )
```

```python
import functools
import math

import jax
import jax.numpy as jnp
from jax import lax
from jax.experimental import pallas as pl
from jax.experimental.pallas import tpu as pltpu
from jax.sharding import PartitionSpec as P

HEADS = 8
HEAD_DIM = 128
LANES = 128
POS_ROWS = 16
HIGH_SHIFT = 7
LOW_MASK = 127

den_low = 1e-18
den_high = 1e37
neg_fill = -1e30
vmem_bytes = 16 * 1024 * 1024


VMEM = pl.BlockSpec(memory_space=pltpu.VMEM)


def call(kernel, out_shape, operands, scratch=(), flops=0):
    size = sum(x.size * x.dtype.itemsize for x in operands)
    return pl.pallas_call(
        kernel,
        out_shape=out_shape,
        in_specs=[VMEM] * len(operands),
        out_specs=jax.tree.map(lambda s: VMEM, out_shape),
        scratch_shapes=scratch,
        compiler_params=pltpu.CompilerParams(vmem_limit_bytes=vmem_bytes),
        cost_estimate=pl.CostEstimate(flops=flops, bytes_accessed=size, transcendentals=0),
    )(*operands)


def pack_kernel(key_ref, value_ref, pos_ref, q_ref, block_ref, qs_ref):
    tokens = key_ref.shape[0]
    block_ref[0, :tokens, :] = key_ref[...]
    block_ref[0, tokens : 2 * tokens, :] = value_ref[...]
    row = lax.broadcasted_iota(jnp.int32, (POS_ROWS, LANES), 0)
    tile = jnp.zeros((POS_ROWS, LANES), jnp.float32)
    for j in range(tokens // LANES):
        pos = pos_ref[:, j * LANES : (j + 1) * LANES]
        high = (pos >> HIGH_SHIFT).astype(jnp.float32)
        low = (pos & LOW_MASK).astype(jnp.float32)
        tile = jnp.where(row == 2 * j, jnp.broadcast_to(high, tile.shape), tile)
        tile = jnp.where(row == 2 * j + 1, jnp.broadcast_to(low, tile.shape), tile)
    block_ref[0, 2 * tokens :, :] = tile.astype(block_ref.dtype)
    for h in range(HEADS):
        qs_ref[h * tokens : (h + 1) * tokens, :] = q_ref[:, h * HEAD_DIM : (h + 1) * HEAD_DIM]


def block_rows(ref):
    return (ref.shape[1] - POS_ROWS) // 2


def keys_of(ref, i):
    return ref[i, : block_rows(ref), :]


def values_of(ref, i):
    rows = block_rows(ref)
    return jnp.concatenate(
        [ref[i, rows : 2 * rows, :], jnp.ones((rows, HEAD_DIM), jnp.bfloat16)], axis=1
    )


def visible_of(ref, i, query_pos):
    rows = block_rows(ref)
    parts = ref[i, 2 * rows :, :].astype(jnp.float32)
    return jnp.concatenate(
        [
            parts[2 * j : 2 * j + 1] * (LOW_MASK + 1) + parts[2 * j + 1 : 2 * j + 2] <= query_pos
            for j in range(rows // LANES)
        ],
        axis=1,
    )


def dot_keys(q, keys):
    return lax.dot_general(
        q, keys, (((1,), (1,)), ((), ())), preferred_element_type=jnp.float32
    )


def absorb(qs_ref, query_pos, total, blocks, at, stack):
    pre = HEAD_DIM ** (-0.5) * math.log2(math.e)
    q = qs_ref[at, :]
    for j in range(0, len(blocks), 2):
        group = blocks[j : j + 2]
        scores = dot_keys(q, jnp.concatenate([keys_of(*b) for b in group], axis=0))
        mask = jnp.concatenate([visible_of(*b, query_pos) for b in group], axis=1)
        mask = jnp.concatenate([mask] * stack, axis=0)
        weights = jnp.where(mask, jnp.exp2(scores * pre), 0.0).astype(jnp.bfloat16)
        part = jnp.dot(
            weights,
            jnp.concatenate([values_of(*b) for b in group], axis=0),
            preferred_element_type=jnp.float32,
        )
        total = part if total is None else total + part
    return total


def accumulate(qs_ref, query_pos, before, after, pieces):
    stack = 4 if HEADS % 4 == 0 else 1
    tokens = query_pos.shape[0]
    span = stack * tokens
    small = sum(p.shape[0] for p in pieces) <= 8
    for r in range(HEADS // stack):
        at = slice(r * span, (r + 1) * span)
        start = None if before is None else before[at, :]
        if small:
            blocks = [(p, i) for p in pieces for i in range(p.shape[0])]
            after[at, :] = absorb(qs_ref, query_pos, start, blocks, at, stack)
            continue
        after[at, :] = jnp.zeros((span, 2 * HEAD_DIM), jnp.float32) if start is None else start
        for p in pieces:

            def pair(i, carry, p=p):
                blocks = [(p, 2 * i), (p, 2 * i + 1)]
                after[at, :] = absorb(qs_ref, query_pos, after[at, :], blocks, at, stack)
                return carry

            lax.fori_loop(0, p.shape[0] // 2, pair, 0)


def bundle(pieces, out_ref):
    at = 0
    for p in pieces:
        out_ref[at : at + p.shape[0]] = p[...]
        at += p.shape[0]


def first_kernel(count, qs_ref, pos_ref, *refs):
    pieces = refs[:count]
    acc_ref, bundle_ref, qpos_ref = refs[count:]
    tokens = pos_ref.shape[1]
    bundle(pieces, bundle_ref)
    qpos_ref[...] = jnp.transpose(
        jnp.broadcast_to(pos_ref[...].astype(jnp.float32), (LANES, tokens))
    )
    accumulate(qs_ref, qpos_ref[...], None, acc_ref, pieces)


def next_kernel(count, qs_ref, qpos_ref, before_ref, *refs):
    pieces = refs[:count]
    if len(refs) > count + 1:
        bundle(pieces, refs[count + 1])
    accumulate(qs_ref, qpos_ref[...], before_ref, refs[count], pieces)


def last_kernel(count, qs_ref, qpos_ref, before_ref, *refs):
    pieces = refs[:count]
    o_ref, acc_ref = refs[count:]
    query_pos = qpos_ref[...]
    tokens = query_pos.shape[0]
    scale = HEAD_DIM ** (-0.5)
    accumulate(qs_ref, query_pos, before_ref, acc_ref, pieces[:1])

    def store():
        for h in range(HEADS):
            part = acc_ref[h * tokens : (h + 1) * tokens, :]
            o_ref[:, h * HEAD_DIM : (h + 1) * HEAD_DIM] = (
                part[:, :HEAD_DIM] / part[:, HEAD_DIM:]
            ).astype(o_ref.dtype)

    store()
    den = acc_ref[:, HEAD_DIM:]
    good = (den >= den_low) & (den <= den_high)

    @pl.when(jnp.min(jnp.where(good, 1.0, 0.0)) < 0.5)
    def _():
        def one_head(h, carry):
            at = pl.ds(pl.multiple_of(h * tokens, tokens), tokens)
            q = qs_ref[at, :]
            top = jnp.full((tokens, 1), neg_fill, jnp.float32)
            for ref in pieces:

                def raise_top(i, top, ref=ref):
                    s = dot_keys(q, keys_of(ref, i)) * scale
                    s = jnp.where(visible_of(ref, i, query_pos), s, neg_fill)
                    return jnp.maximum(top, jnp.max(s, axis=1, keepdims=True))

                top = lax.fori_loop(0, ref.shape[0], raise_top, top)
            total = jnp.zeros((tokens, 2 * HEAD_DIM), jnp.float32)
            for ref in pieces:

                def add(i, total, ref=ref):
                    s = dot_keys(q, keys_of(ref, i)) * scale
                    w = jnp.where(visible_of(ref, i, query_pos), jnp.exp(s - top), 0.0)
                    return total + jnp.dot(
                        w.astype(jnp.bfloat16),
                        values_of(ref, i),
                        preferred_element_type=jnp.float32,
                    )

                total = lax.fori_loop(0, ref.shape[0], add, total)
            acc_ref[at, :] = total
            return carry

        lax.fori_loop(0, HEADS, one_head, 0)
        store()


def swap(x, axis, size, bit):
    return lax.ppermute(x, axis, [(i, i ^ bit) for i in range(size)])


def attention(rows, cols, queries, keys, values, positions):
    tokens = queries.shape[0]
    pos = positions.reshape(1, tokens)
    block = jax.ShapeDtypeStruct((1, 2 * tokens + POS_ROWS, HEAD_DIM), jnp.bfloat16)
    in_hbm = functools.partial(pltpu.with_memory_space_constraint, memory_space=pltpu.HBM)
    own, qs = call(
        pack_kernel,
        (block, jax.ShapeDtypeStruct((HEADS * tokens, HEAD_DIM), jnp.bfloat16)),
        [in_hbm(x) for x in (keys, values, pos, queries)],
    )
    acc = jax.ShapeDtypeStruct((HEADS * tokens, 2 * HEAD_DIM), jnp.float32)
    qpos = jax.ShapeDtypeStruct((tokens, LANES), jnp.float32)

    def bundled(pieces):
        return jax.ShapeDtypeStruct(
            (sum(p.shape[0] for p in pieces),) + pieces[0].shape[1:], jnp.bfloat16
        )

    def work(pieces):
        return 4 * HEADS * tokens * HEAD_DIM * tokens * sum(p.shape[0] for p in pieces)

    def further(before, pieces, with_bundle):
        out = (acc, bundled(pieces)) if with_bundle else (acc,)
        return call(
            functools.partial(next_kernel, len(pieces)), out,
            [qs, query_pos, before, *pieces], flops=work(pieces),
        )

    bit = rows // 2
    while bit >= 4:
        own = jnp.concatenate([own, swap(own, "rows", rows, bit)], axis=0)
        bit //= 2
    z2 = swap(own, "rows", rows, 2)
    z1 = swap(own, "rows", rows, 1)
    xo = swap(own, "cols", cols, 2)
    z3 = swap(z2, "rows", rows, 1)
    xz2 = swap(z2, "cols", cols, 2)
    xz1 = swap(z1, "cols", cols, 2)
    near = [own, z2, z1, xo]
    acc1, b1, query_pos = call(
        functools.partial(first_kernel, len(near)),
        (acc, bundled(near), qpos),
        [qs, pos, *near], flops=work(near),
    )
    xz3 = swap(z3, "cols", cols, 2)
    cb1 = swap(b1, "cols", cols, 1)
    acc2, b2 = further(acc1, [z3, xz2, xz1], True)
    cb2 = swap(b2, "cols", cols, 1)
    (acc3,) = further(acc2, [cb1], False)
    c3 = swap(xz3, "cols", cols, 1)
    (acc4,) = further(acc3, [cb2, xz3], False)
    pieces = [c3, b1, b2, xz3, cb1, cb2]
    return call(
        functools.partial(last_kernel, len(pieces)),
        jax.ShapeDtypeStruct(queries.shape, jnp.bfloat16),
        [qs, query_pos, acc4, *pieces],
        scratch=[pltpu.VMEM(acc.shape, acc.dtype)], flops=work([c3]),
    )


def solution(mesh):
    rows, cols = mesh.shape["rows"], mesh.shape["cols"]

    def shards(*arrays):
        return attention(rows, cols, *arrays)

    return jax.shard_map(
        shards,
        mesh=mesh,
        in_specs=(
            P(("groups", "rows", "cols"), None),
            P(("groups", "rows", "cols"), None),
            P(("groups", "rows", "cols"), None),
            P(("groups", "rows", "cols")),
        ),
        out_specs=P(("groups", "rows", "cols"), None),
        check_vma=False,
    )
```

```python
import functools
import math

import jax
import jax.numpy as jnp
from jax import lax
from jax.experimental import pallas as pl
from jax.experimental.pallas import tpu as pltpu
from jax.sharding import PartitionSpec as P

HEADS = 8
HEAD_DIM = 128
LANES = 128
POS_ROWS = 16
HIGH_SHIFT = 7
LOW_MASK = 127

den_low = 1e-18
den_high = 1e37
neg_fill = -1e30
vmem_bytes = 16 * 1024 * 1024


VMEM = pl.BlockSpec(memory_space=pltpu.VMEM)


def call(kernel, out_shape, operands, scratch=(), flops=0, out_spec=VMEM):
    size = sum(x.size * x.dtype.itemsize for x in operands)
    return pl.pallas_call(
        kernel,
        out_shape=out_shape,
        in_specs=[VMEM] * len(operands),
        out_specs=jax.tree.map(lambda s: out_spec, out_shape),
        scratch_shapes=scratch,
        compiler_params=pltpu.CompilerParams(vmem_limit_bytes=vmem_bytes),
        cost_estimate=pl.CostEstimate(flops=flops, bytes_accessed=size, transcendentals=0),
    )(*operands)


def pack_kernel(key_ref, value_ref, pos_ref, q_ref, block_ref, qs_ref):
    tokens = key_ref.shape[0]
    block_ref[0, :tokens, :] = key_ref[...]
    block_ref[0, tokens : 2 * tokens, :] = value_ref[...]
    row = lax.broadcasted_iota(jnp.int32, (POS_ROWS, LANES), 0)
    tile = jnp.zeros((POS_ROWS, LANES), jnp.float32)
    for j in range(tokens // LANES):
        pos = pos_ref[:, j * LANES : (j + 1) * LANES]
        high = (pos >> HIGH_SHIFT).astype(jnp.float32)
        low = (pos & LOW_MASK).astype(jnp.float32)
        tile = jnp.where(row == 2 * j, jnp.broadcast_to(high, tile.shape), tile)
        tile = jnp.where(row == 2 * j + 1, jnp.broadcast_to(low, tile.shape), tile)
    block_ref[0, 2 * tokens :, :] = tile.astype(block_ref.dtype)
    for h in range(HEADS):
        qs_ref[h * tokens : (h + 1) * tokens, :] = q_ref[:, h * HEAD_DIM : (h + 1) * HEAD_DIM]


def block_rows(ref):
    return (ref.shape[1] - POS_ROWS) // 2


def keys_of(ref, i):
    return ref[i, : block_rows(ref), :]


def values_of(ref, i):
    rows = block_rows(ref)
    return jnp.concatenate(
        [ref[i, rows : 2 * rows, :], jnp.ones((rows, HEAD_DIM), jnp.bfloat16)], axis=1
    )


def visible_of(ref, i, query_pos):
    rows = block_rows(ref)
    parts = ref[i, 2 * rows :, :].astype(jnp.float32)
    return jnp.concatenate(
        [
            parts[2 * j : 2 * j + 1] * (LOW_MASK + 1) + parts[2 * j + 1 : 2 * j + 2] <= query_pos
            for j in range(rows // LANES)
        ],
        axis=1,
    )


def dot_keys(q, keys):
    return lax.dot_general(
        q, keys, (((1,), (1,)), ((), ())), preferred_element_type=jnp.float32
    )


def absorb(qs_ref, query_pos, total, blocks, at, stack):
    pre = HEAD_DIM ** (-0.5) * math.log2(math.e)
    q = qs_ref[at, :]
    for j in range(0, len(blocks), 2):
        group = blocks[j : j + 2]
        scores = dot_keys(q, jnp.concatenate([keys_of(*b) for b in group], axis=0))
        mask = jnp.concatenate([visible_of(*b, query_pos) for b in group], axis=1)
        mask = jnp.concatenate([mask] * stack, axis=0)
        weights = jnp.where(mask, jnp.exp2(scores * pre), 0.0).astype(jnp.bfloat16)
        part = jnp.dot(
            weights,
            jnp.concatenate([values_of(*b) for b in group], axis=0),
            preferred_element_type=jnp.float32,
        )
        total = part if total is None else total + part
    return total


def accumulate(qs_ref, query_pos, before, after, pieces, groups=None):
    stack = 4 if HEADS % 4 == 0 else 1
    tokens = query_pos.shape[0]
    span = stack * tokens
    small = sum(p.shape[0] for p in pieces) <= 8
    for r in groups or range(HEADS // stack):
        at = slice(r * span, (r + 1) * span)
        start = None if before is None else before[at, :]
        if small:
            blocks = [(p, i) for p in pieces for i in range(p.shape[0])]
            after[at, :] = absorb(qs_ref, query_pos, start, blocks, at, stack)
            continue
        after[at, :] = jnp.zeros((span, 2 * HEAD_DIM), jnp.float32) if start is None else start
        for p in pieces:

            def pair(i, carry, p=p):
                blocks = [(p, 2 * i), (p, 2 * i + 1)]
                after[at, :] = absorb(qs_ref, query_pos, after[at, :], blocks, at, stack)
                return carry

            lax.fori_loop(0, p.shape[0] // 2, pair, 0)


def bundle(pieces, out_ref):
    at = 0
    for p in pieces:
        out_ref[at : at + p.shape[0]] = p[...]
        at += p.shape[0]


def first_kernel(count, qs_ref, pos_ref, *refs):
    pieces = refs[:count]
    acc_ref, bundle_ref, qpos_ref = refs[count:]
    tokens = pos_ref.shape[1]
    bundle(pieces, bundle_ref)
    qpos_ref[...] = jnp.transpose(
        jnp.broadcast_to(pos_ref[...].astype(jnp.float32), (LANES, tokens))
    )
    accumulate(qs_ref, qpos_ref[...], None, acc_ref, pieces)


def next_kernel(count, qs_ref, qpos_ref, before_ref, *refs):
    pieces = refs[:count]
    if len(refs) > count + 1:
        bundle(pieces, refs[count + 1])
    accumulate(qs_ref, qpos_ref[...], before_ref, refs[count], pieces)


def last_kernel(count, qs_ref, qpos_ref, before_ref, *refs):
    pieces = refs[:-4]
    o_ref, acc_ref, out_ref, sems = refs[-4:]
    query_pos = qpos_ref[...]
    tokens = query_pos.shape[0]
    scale = HEAD_DIM ** (-0.5)
    stack = 4 if HEADS % 4 == 0 else 1

    def copy(r):
        at = slice(r * stack * HEAD_DIM, (r + 1) * stack * HEAD_DIM)
        return pltpu.make_async_copy(out_ref.at[:, at], o_ref.at[:, at], sems.at[r])

    def divide(r):
        for h in range(r * stack, (r + 1) * stack):
            part = acc_ref[h * tokens : (h + 1) * tokens, :]
            out_ref[:, h * HEAD_DIM : (h + 1) * HEAD_DIM] = (
                part[:, :HEAD_DIM] / part[:, HEAD_DIM:]
            ).astype(out_ref.dtype)

    groups = range(HEADS // stack)
    for r in groups:
        accumulate(qs_ref, query_pos, before_ref, acc_ref, pieces[:count], (r,))
        divide(r)
        copy(r).start()
    den = acc_ref[:, HEAD_DIM:]
    good = (den >= den_low) & (den <= den_high)
    worst = jnp.min(jnp.where(good, 1.0, 0.0))
    for r in groups:
        copy(r).wait()

    @pl.when(worst < 0.5)
    def _():
        def one_head(h, carry):
            at = pl.ds(pl.multiple_of(h * tokens, tokens), tokens)
            q = qs_ref[at, :]
            top = jnp.full((tokens, 1), neg_fill, jnp.float32)
            for ref in pieces:

                def raise_top(i, top, ref=ref):
                    s = dot_keys(q, keys_of(ref, i)) * scale
                    s = jnp.where(visible_of(ref, i, query_pos), s, neg_fill)
                    return jnp.maximum(top, jnp.max(s, axis=1, keepdims=True))

                top = lax.fori_loop(0, ref.shape[0], raise_top, top)
            total = jnp.zeros((tokens, 2 * HEAD_DIM), jnp.float32)
            for ref in pieces:

                def add(i, total, ref=ref):
                    s = dot_keys(q, keys_of(ref, i)) * scale
                    w = jnp.where(visible_of(ref, i, query_pos), jnp.exp(s - top), 0.0)
                    return total + jnp.dot(
                        w.astype(jnp.bfloat16),
                        values_of(ref, i),
                        preferred_element_type=jnp.float32,
                    )

                total = lax.fori_loop(0, ref.shape[0], add, total)
            acc_ref[at, :] = total
            return carry

        lax.fori_loop(0, HEADS, one_head, 0)
        for r in groups:
            divide(r)
            copy(r).start()
        for r in groups:
            copy(r).wait()


def swap(x, axis, size, bit):
    return lax.ppermute(x, axis, [(i, i ^ bit) for i in range(size)])


def attention(rows, cols, queries, keys, values, positions):
    tokens = queries.shape[0]
    pos = positions.reshape(1, tokens)
    block = jax.ShapeDtypeStruct((1, 2 * tokens + POS_ROWS, HEAD_DIM), jnp.bfloat16)
    in_hbm = functools.partial(pltpu.with_memory_space_constraint, memory_space=pltpu.HBM)
    own, qs = call(
        pack_kernel,
        (block, jax.ShapeDtypeStruct((HEADS * tokens, HEAD_DIM), jnp.bfloat16)),
        [in_hbm(x) for x in (keys, values, pos, queries)],
    )
    acc = jax.ShapeDtypeStruct((HEADS * tokens, 2 * HEAD_DIM), jnp.float32)
    qpos = jax.ShapeDtypeStruct((tokens, LANES), jnp.float32)

    def bundled(pieces):
        return jax.ShapeDtypeStruct(
            (sum(p.shape[0] for p in pieces),) + pieces[0].shape[1:], jnp.bfloat16
        )

    def work(pieces):
        return 4 * HEADS * tokens * HEAD_DIM * tokens * sum(p.shape[0] for p in pieces)

    def further(before, pieces, with_bundle):
        out = (acc, bundled(pieces)) if with_bundle else (acc,)
        return call(
            functools.partial(next_kernel, len(pieces)), out,
            [qs, query_pos, before, *pieces], flops=work(pieces),
        )

    bit = rows // 2
    while bit >= 4:
        own = jnp.concatenate([own, swap(own, "rows", rows, bit)], axis=0)
        bit //= 2
    z2 = swap(own, "rows", rows, 2)
    z1 = swap(own, "rows", rows, 1)
    xo = swap(own, "cols", cols, 2)
    z3 = swap(z2, "rows", rows, 1)
    xz2 = swap(z2, "cols", cols, 2)
    xz1 = swap(z1, "cols", cols, 2)
    near = [own, z2, z1, xo]
    acc1, b1, query_pos = call(
        functools.partial(first_kernel, len(near)),
        (acc, bundled(near), qpos),
        [qs, pos, *near], flops=work(near),
    )
    xz3 = swap(z3, "cols", cols, 2)
    cb1 = swap(b1, "cols", cols, 1)
    acc2, b2 = further(acc1, [z3, xz2], True)
    cb2 = swap(b2, "cols", cols, 1)
    cx1 = swap(xz1, "cols", cols, 1)
    (acc3,) = further(acc2, [cb1], False)
    c3 = swap(xz3, "cols", cols, 1)
    (acc4,) = further(acc3, [cb2, cx1, xz1], False)
    pieces = [xz3, c3, b1, b2, xz1, cb1, cb2, cx1]
    return call(
        functools.partial(last_kernel, 2),
        jax.ShapeDtypeStruct(queries.shape, jnp.bfloat16),
        [qs, query_pos, acc4, *pieces],
        scratch=[
            pltpu.VMEM(acc.shape, acc.dtype),
            pltpu.VMEM(queries.shape, jnp.bfloat16),
            pltpu.SemaphoreType.DMA((HEADS,)),
        ],
        flops=work([c3]), out_spec=pl.BlockSpec(memory_space=pltpu.HBM),
    )


def solution(mesh):
    rows, cols = mesh.shape["rows"], mesh.shape["cols"]

    def shards(*arrays):
        return attention(rows, cols, *arrays)

    return jax.shard_map(
        shards,
        mesh=mesh,
        in_specs=(
            P(("groups", "rows", "cols"), None),
            P(("groups", "rows", "cols"), None),
            P(("groups", "rows", "cols"), None),
            P(("groups", "rows", "cols")),
        ),
        out_specs=P(("groups", "rows", "cols"), None),
        check_vma=False,
    )
```

```python
import functools
import math

import jax
import jax.numpy as jnp
from jax import lax
from jax.experimental import pallas as pl
from jax.experimental.pallas import tpu as pltpu
from jax.sharding import PartitionSpec as P

HEADS = 8
HEAD_DIM = 128
LANES = 128
POS_ROWS = 16
HIGH_SHIFT = 7
LOW_MASK = 127

den_low = 1e-18
den_high = 1e37
neg_fill = -1e30
vmem_bytes = 16 * 1024 * 1024


VMEM = pl.BlockSpec(memory_space=pltpu.VMEM)


def call(kernel, out_shape, operands, scratch=(), flops=0, out_spec=VMEM):
    size = sum(x.size * x.dtype.itemsize for x in operands)
    return pl.pallas_call(
        kernel,
        out_shape=out_shape,
        in_specs=[VMEM] * len(operands),
        out_specs=jax.tree.map(lambda s: out_spec, out_shape),
        scratch_shapes=scratch,
        compiler_params=pltpu.CompilerParams(vmem_limit_bytes=vmem_bytes),
        cost_estimate=pl.CostEstimate(flops=flops, bytes_accessed=size, transcendentals=0),
    )(*operands)


def pack_kernel(key_ref, value_ref, pos_ref, block_ref, near_pos_ref):
    tokens = key_ref.shape[0]
    near_pos_ref[...] = pos_ref[...].astype(jnp.float32)
    block_ref[0, :tokens, :] = key_ref[...]
    block_ref[0, tokens : 2 * tokens, :] = value_ref[...]
    row = lax.broadcasted_iota(jnp.int32, (POS_ROWS, LANES), 0)
    tile = jnp.zeros((POS_ROWS, LANES), jnp.float32)
    for j in range(tokens // LANES):
        pos = pos_ref[:, j * LANES : (j + 1) * LANES]
        high = (pos >> HIGH_SHIFT).astype(jnp.float32)
        low = (pos & LOW_MASK).astype(jnp.float32)
        tile = jnp.where(row == 2 * j, jnp.broadcast_to(high, tile.shape), tile)
        tile = jnp.where(row == 2 * j + 1, jnp.broadcast_to(low, tile.shape), tile)
    block_ref[0, 2 * tokens :, :] = tile.astype(block_ref.dtype)


def block_rows(ref):
    return (ref.shape[1] - POS_ROWS) // 2


def keys_of(ref, i):
    return ref[i, : block_rows(ref), :]


def values_of(ref, i):
    rows = block_rows(ref)
    return jnp.concatenate(
        [ref[i, rows : 2 * rows, :], jnp.ones((rows, HEAD_DIM), jnp.bfloat16)], axis=1
    )


def visible_of(ref, i, query_pos):
    rows = block_rows(ref)
    parts = ref[i, 2 * rows :, :].astype(jnp.float32)
    return jnp.concatenate(
        [
            parts[2 * j : 2 * j + 1] * (LOW_MASK + 1) + parts[2 * j + 1 : 2 * j + 2] <= query_pos
            for j in range(rows // LANES)
        ],
        axis=1,
    )


def dot_keys(q, keys):
    return lax.dot_general(
        q, keys, (((1,), (1,)), ((), ())), preferred_element_type=jnp.float32
    )


def absorb(qs_ref, query_pos, total, blocks, at, stack):
    pre = HEAD_DIM ** (-0.5) * math.log2(math.e)
    q = qs_ref[at, :]
    for j in range(0, len(blocks), 2):
        group = blocks[j : j + 2]
        scores = dot_keys(q, jnp.concatenate([keys_of(*b) for b in group], axis=0))
        mask = jnp.concatenate([visible_of(*b, query_pos) for b in group], axis=1)
        mask = jnp.concatenate([mask] * stack, axis=0)
        weights = jnp.where(mask, jnp.exp2(scores * pre), 0.0).astype(jnp.bfloat16)
        part = jnp.dot(
            weights,
            jnp.concatenate([values_of(*b) for b in group], axis=0),
            preferred_element_type=jnp.float32,
        )
        total = part if total is None else total + part
    return total


def accumulate(qs_ref, query_pos, before, after, pieces, groups=None):
    stack = 4 if HEADS % 4 == 0 else 1
    tokens = query_pos.shape[0]
    span = stack * tokens
    small = sum(p.shape[0] for p in pieces) <= 8
    for r in groups or range(HEADS // stack):
        at = slice(r * span, (r + 1) * span)
        start = None if before is None else before[at, :]
        if small:
            blocks = [(p, i) for p in pieces for i in range(p.shape[0])]
            after[at, :] = absorb(qs_ref, query_pos, start, blocks, at, stack)
            continue
        after[at, :] = jnp.zeros((span, 2 * HEAD_DIM), jnp.float32) if start is None else start
        for p in pieces:

            def pair(i, carry, p=p):
                blocks = [(p, 2 * i), (p, 2 * i + 1)]
                after[at, :] = absorb(qs_ref, query_pos, after[at, :], blocks, at, stack)
                return carry

            lax.fori_loop(0, p.shape[0] // 2, pair, 0)


def bundle(pieces, out_ref):
    at = 0
    for p in pieces:
        out_ref[at : at + p.shape[0]] = p[...]
        at += p.shape[0]


def bundle_kernel(groups, *refs):
    for group, out_ref in zip(groups, refs[-len(groups) :]):
        bundle([refs[i] for i in group], out_ref)


def first_kernel(count, q_ref, pos_ref, *refs):
    acc_ref, qpos_ref, qs_ref = refs[count:]
    tokens = pos_ref.shape[1]
    for h in range(HEADS):
        qs_ref[h * tokens : (h + 1) * tokens, :] = q_ref[:, h * HEAD_DIM : (h + 1) * HEAD_DIM]
    qpos_ref[...] = jnp.transpose(
        jnp.broadcast_to(pos_ref[...], (LANES, tokens))
    )
    accumulate(qs_ref, qpos_ref[...], None, acc_ref, refs[:count])


def next_kernel(count, qs_ref, qpos_ref, before_ref, *refs):
    accumulate(qs_ref, qpos_ref[...], before_ref, refs[count], refs[:count])


def last_kernel(count, qs_ref, qpos_ref, before_ref, *refs):
    pieces = refs[:-4]
    o_ref, acc_ref, out_ref, sems = refs[-4:]
    query_pos = qpos_ref[...]
    tokens = query_pos.shape[0]
    scale = HEAD_DIM ** (-0.5)
    stack = 4 if HEADS % 4 == 0 else 1

    def copy(r):
        at = slice(r * stack * HEAD_DIM, (r + 1) * stack * HEAD_DIM)
        return pltpu.make_async_copy(out_ref.at[:, at], o_ref.at[:, at], sems.at[r])

    def divide(r):
        for h in range(r * stack, (r + 1) * stack):
            part = acc_ref[h * tokens : (h + 1) * tokens, :]
            out_ref[:, h * HEAD_DIM : (h + 1) * HEAD_DIM] = (
                part[:, :HEAD_DIM] / part[:, HEAD_DIM:]
            ).astype(out_ref.dtype)

    groups = range(HEADS // stack)
    for r in groups:
        accumulate(qs_ref, query_pos, before_ref, acc_ref, pieces[:count], (r,))
        divide(r)
        copy(r).start()
    den = acc_ref[:, HEAD_DIM:]
    good = (den >= den_low) & (den <= den_high)
    worst = jnp.min(jnp.where(good, 1.0, 0.0))
    for r in groups:
        copy(r).wait()

    @pl.when(worst < 0.5)
    def _():
        def one_head(h, carry):
            at = pl.ds(pl.multiple_of(h * tokens, tokens), tokens)
            q = qs_ref[at, :]
            top = jnp.full((tokens, 1), neg_fill, jnp.float32)
            for ref in pieces:

                def raise_top(i, top, ref=ref):
                    s = dot_keys(q, keys_of(ref, i)) * scale
                    s = jnp.where(visible_of(ref, i, query_pos), s, neg_fill)
                    return jnp.maximum(top, jnp.max(s, axis=1, keepdims=True))

                top = lax.fori_loop(0, ref.shape[0], raise_top, top)
            total = jnp.zeros((tokens, 2 * HEAD_DIM), jnp.float32)
            for ref in pieces:

                def add(i, total, ref=ref):
                    s = dot_keys(q, keys_of(ref, i)) * scale
                    w = jnp.where(visible_of(ref, i, query_pos), jnp.exp(s - top), 0.0)
                    return total + jnp.dot(
                        w.astype(jnp.bfloat16),
                        values_of(ref, i),
                        preferred_element_type=jnp.float32,
                    )

                total = lax.fori_loop(0, ref.shape[0], add, total)
            acc_ref[at, :] = total
            return carry

        lax.fori_loop(0, HEADS, one_head, 0)
        for r in groups:
            divide(r)
            copy(r).start()
        for r in groups:
            copy(r).wait()


def hop(x, rows, cols, row_bit, col_bit):
    pairs = [
        (r * cols + c, (r ^ row_bit) * cols + (c ^ col_bit)) for r in range(rows) for c in range(cols)
    ]
    return lax.ppermute(x, ("rows", "cols"), pairs)


def swap(x, axis, size, bit):
    return lax.ppermute(x, axis, [(i, i ^ bit) for i in range(size)])


def attention(rows, cols, queries, keys, values, positions):
    tokens = queries.shape[0]
    pos = positions.reshape(1, tokens)
    block = jax.ShapeDtypeStruct((1, 2 * tokens + POS_ROWS, HEAD_DIM), jnp.bfloat16)
    in_hbm = functools.partial(pltpu.with_memory_space_constraint, memory_space=pltpu.HBM)
    own, near_pos = call(
        pack_kernel,
        (
            block,
            jax.ShapeDtypeStruct((1, tokens), jnp.float32),
        ),
        [in_hbm(x) for x in (keys, values, pos)],
    )
    acc = jax.ShapeDtypeStruct((HEADS * tokens, 2 * HEAD_DIM), jnp.float32)
    qpos = jax.ShapeDtypeStruct((tokens, LANES), jnp.float32)
    heads = jax.ShapeDtypeStruct((HEADS * tokens, HEAD_DIM), jnp.bfloat16)

    def together(pieces, *groups):
        shapes = tuple(
            jax.ShapeDtypeStruct(
                (sum(pieces[i].shape[0] for i in g),) + pieces[0].shape[1:], jnp.bfloat16
            )
            for g in groups
        )
        return call(functools.partial(bundle_kernel, groups), shapes, pieces)

    def work(pieces):
        return 4 * HEADS * tokens * HEAD_DIM * tokens * sum(p.shape[0] for p in pieces)

    def further(before, pieces):
        return call(
            functools.partial(next_kernel, len(pieces)), acc,
            [qs, query_pos, before, *pieces], flops=work(pieces),
        )

    bit = rows // 2
    while bit >= 4:
        own = jnp.concatenate([own, swap(own, "rows", rows, bit)], axis=0)
        bit //= 2
    z2 = hop(own, rows, cols, 2, 0)
    z1 = hop(own, rows, cols, 1, 0)
    xo = hop(own, rows, cols, 0, 2)
    xz3 = hop(z2, rows, cols, 1, 2)
    xz2 = hop(z2, rows, cols, 0, 2)
    b12, b1 = together([own, z2, z1, xo], (1, 3), (0, 1, 2, 3))
    zb = hop(b12, rows, cols, 1, 0)
    cb1 = swap(b1, "cols", cols, 1)
    acc1, query_pos, qs = call(
        functools.partial(first_kernel, 1), (acc, qpos, heads), [in_hbm(queries), near_pos, b1], flops=work([b1])
    )
    (b2,) = together([xz3, xz2], (0, 1))
    cb2 = swap(b2, "cols", cols, 1)
    acc2 = further(acc1, [cb1, b2])
    czb = swap(zb, "cols", cols, 1)
    acc4 = further(acc2, [cb2, zb])
    pieces = [czb, b1, cb1, b2, cb2, zb]
    return call(
        functools.partial(last_kernel, 1),
        jax.ShapeDtypeStruct(queries.shape, jnp.bfloat16),
        [qs, query_pos, acc4, *pieces],
        scratch=[
            pltpu.VMEM(acc.shape, acc.dtype),
            pltpu.VMEM(queries.shape, jnp.bfloat16),
            pltpu.SemaphoreType.DMA((HEADS,)),
        ],
        flops=work([czb]), out_spec=pl.BlockSpec(memory_space=pltpu.HBM),
    )


def solution(mesh):
    rows, cols = mesh.shape["rows"], mesh.shape["cols"]

    def shards(*arrays):
        return attention(rows, cols, *arrays)

    return jax.shard_map(
        shards,
        mesh=mesh,
        in_specs=(
            P(("groups", "rows", "cols"), None),
            P(("groups", "rows", "cols"), None),
            P(("groups", "rows", "cols"), None),
            P(("groups", "rows", "cols")),
        ),
        out_specs=P(("groups", "rows", "cols"), None),
        check_vma=False,
    )
```

```python
import functools
import math

import jax
import jax.numpy as jnp
from jax import lax
from jax.experimental import pallas as pl
from jax.experimental.pallas import tpu as pltpu
from jax.sharding import PartitionSpec as P

HEADS = 8
HEAD_DIM = 128
LANES = 128
POS_ROWS = 16
HIGH_SHIFT = 7
LOW_MASK = 127

den_low = 1e-18
den_high = 1e37
neg_fill = -1e30
vmem_bytes = 16 * 1024 * 1024


VMEM = pl.BlockSpec(memory_space=pltpu.VMEM)


def call(kernel, out_shape, operands, scratch=(), flops=0, out_spec=VMEM):
    size = sum(x.size * x.dtype.itemsize for x in operands)
    return pl.pallas_call(
        kernel,
        out_shape=out_shape,
        in_specs=[VMEM] * len(operands),
        out_specs=jax.tree.map(lambda s: out_spec, out_shape),
        scratch_shapes=scratch,
        compiler_params=pltpu.CompilerParams(vmem_limit_bytes=vmem_bytes),
        cost_estimate=pl.CostEstimate(flops=flops, bytes_accessed=size, transcendentals=0),
    )(*operands)


def pack_kernel(key_ref, value_ref, pos_ref, block_ref, near_pos_ref):
    tokens = key_ref.shape[0]
    near_pos_ref[...] = pos_ref[...].astype(jnp.float32)
    block_ref[0, :tokens, :] = key_ref[...]
    block_ref[0, tokens : 2 * tokens, :] = value_ref[...]
    row = lax.broadcasted_iota(jnp.int32, (POS_ROWS, LANES), 0)
    tile = jnp.zeros((POS_ROWS, LANES), jnp.float32)
    for j in range(tokens // LANES):
        pos = pos_ref[:, j * LANES : (j + 1) * LANES]
        high = (pos >> HIGH_SHIFT).astype(jnp.float32)
        low = (pos & LOW_MASK).astype(jnp.float32)
        tile = jnp.where(row == 2 * j, jnp.broadcast_to(high, tile.shape), tile)
        tile = jnp.where(row == 2 * j + 1, jnp.broadcast_to(low, tile.shape), tile)
    block_ref[0, 2 * tokens :, :] = tile.astype(block_ref.dtype)


def block_rows(ref):
    return (ref.shape[1] - POS_ROWS) // 2


def keys_of(ref, i):
    return ref[i, : block_rows(ref), :]


def values_of(ref, i):
    rows = block_rows(ref)
    return jnp.concatenate(
        [ref[i, rows : 2 * rows, :], jnp.ones((rows, HEAD_DIM), jnp.bfloat16)], axis=1
    )


def visible_of(ref, i, query_pos):
    rows = block_rows(ref)
    parts = ref[i, 2 * rows :, :].astype(jnp.float32)
    return jnp.concatenate(
        [
            parts[2 * j : 2 * j + 1] * (LOW_MASK + 1) + parts[2 * j + 1 : 2 * j + 2] <= query_pos
            for j in range(rows // LANES)
        ],
        axis=1,
    )


def dot_keys(q, keys):
    return lax.dot_general(
        q, keys, (((1,), (1,)), ((), ())), preferred_element_type=jnp.float32
    )


def absorb(qs_ref, query_pos, total, blocks, at, stack):
    pre = HEAD_DIM ** (-0.5) * math.log2(math.e)
    q = qs_ref[at, :]
    for j in range(0, len(blocks), 2):
        group = blocks[j : j + 2]
        scores = dot_keys(q, jnp.concatenate([keys_of(*b) for b in group], axis=0))
        mask = jnp.concatenate([visible_of(*b, query_pos) for b in group], axis=1)
        mask = jnp.concatenate([mask] * stack, axis=0)
        weights = jnp.where(mask, jnp.exp2(scores * pre), 0.0).astype(jnp.bfloat16)
        part = jnp.dot(
            weights,
            jnp.concatenate([values_of(*b) for b in group], axis=0),
            preferred_element_type=jnp.float32,
        )
        total = part if total is None else total + part
    return total


def accumulate(qs_ref, query_pos, before, after, pieces, groups=None):
    stack = 4 if HEADS % 4 == 0 else 1
    tokens = query_pos.shape[0]
    span = stack * tokens
    small = sum(p.shape[0] for p in pieces) <= 8
    for r in groups or range(HEADS // stack):
        at = slice(r * span, (r + 1) * span)
        start = None if before is None else before[at, :]
        if small:
            blocks = [(p, i) for p in pieces for i in range(p.shape[0])]
            after[at, :] = absorb(qs_ref, query_pos, start, blocks, at, stack)
            continue
        after[at, :] = jnp.zeros((span, 2 * HEAD_DIM), jnp.float32) if start is None else start
        for p in pieces:

            def pair(i, carry, p=p):
                blocks = [(p, 2 * i), (p, 2 * i + 1)]
                after[at, :] = absorb(qs_ref, query_pos, after[at, :], blocks, at, stack)
                return carry

            lax.fori_loop(0, p.shape[0] // 2, pair, 0)


def bundle(pieces, out_ref):
    at = 0
    for p in pieces:
        out_ref[at : at + p.shape[0]] = p[...]
        at += p.shape[0]


def bundle_kernel(groups, *refs):
    for group, out_ref in zip(groups, refs[-len(groups) :]):
        bundle([refs[i] for i in group], out_ref)


def first_kernel(count, q_ref, pos_ref, *refs):
    acc_ref, qpos_ref, qs_ref = refs[count:]
    tokens = pos_ref.shape[1]
    for h in range(HEADS):
        qs_ref[h * tokens : (h + 1) * tokens, :] = q_ref[:, h * HEAD_DIM : (h + 1) * HEAD_DIM]
    qpos_ref[...] = jnp.transpose(
        jnp.broadcast_to(pos_ref[...], (LANES, tokens))
    )
    accumulate(qs_ref, qpos_ref[...], None, acc_ref, refs[:count])


def next_kernel(count, qs_ref, qpos_ref, before_ref, *refs):
    accumulate(qs_ref, qpos_ref[...], before_ref, refs[count], refs[:count])


def last_kernel(count, qs_ref, qpos_ref, before_ref, *refs):
    pieces = refs[:-4]
    o_ref, acc_ref, out_ref, sems = refs[-4:]
    query_pos = qpos_ref[...]
    tokens = query_pos.shape[0]
    scale = HEAD_DIM ** (-0.5)
    stack = 4 if HEADS % 4 == 0 else 1

    def copy(r):
        at = slice(r * stack * HEAD_DIM, (r + 1) * stack * HEAD_DIM)
        return pltpu.make_async_copy(out_ref.at[:, at], o_ref.at[:, at], sems.at[r])

    def divide(r):
        for h in range(r * stack, (r + 1) * stack):
            part = acc_ref[h * tokens : (h + 1) * tokens, :]
            out_ref[:, h * HEAD_DIM : (h + 1) * HEAD_DIM] = (
                part[:, :HEAD_DIM] / part[:, HEAD_DIM:]
            ).astype(out_ref.dtype)

    groups = range(HEADS // stack)
    for r in groups:
        accumulate(qs_ref, query_pos, before_ref, acc_ref, pieces[:count], (r,))
        divide(r)
        copy(r).start()
    den = acc_ref[:, HEAD_DIM:]
    good = (den >= den_low) & (den <= den_high)
    worst = jnp.min(jnp.where(good, 1.0, 0.0))
    for r in groups:
        copy(r).wait()

    @pl.when(worst < 0.5)
    def _():
        def one_head(h, carry):
            at = pl.ds(pl.multiple_of(h * tokens, tokens), tokens)
            q = qs_ref[at, :]
            top = jnp.full((tokens, 1), neg_fill, jnp.float32)
            for ref in pieces:

                def raise_top(i, top, ref=ref):
                    s = dot_keys(q, keys_of(ref, i)) * scale
                    s = jnp.where(visible_of(ref, i, query_pos), s, neg_fill)
                    return jnp.maximum(top, jnp.max(s, axis=1, keepdims=True))

                top = lax.fori_loop(0, ref.shape[0], raise_top, top)
            total = jnp.zeros((tokens, 2 * HEAD_DIM), jnp.float32)
            for ref in pieces:

                def add(i, total, ref=ref):
                    s = dot_keys(q, keys_of(ref, i)) * scale
                    w = jnp.where(visible_of(ref, i, query_pos), jnp.exp(s - top), 0.0)
                    return total + jnp.dot(
                        w.astype(jnp.bfloat16),
                        values_of(ref, i),
                        preferred_element_type=jnp.float32,
                    )

                total = lax.fori_loop(0, ref.shape[0], add, total)
            acc_ref[at, :] = total
            return carry

        lax.fori_loop(0, HEADS, one_head, 0)
        for r in groups:
            divide(r)
            copy(r).start()
        for r in groups:
            copy(r).wait()


def hop(x, rows, cols, row_bit, col_bit):
    pairs = [
        (r * cols + c, (r ^ row_bit) * cols + (c ^ col_bit)) for r in range(rows) for c in range(cols)
    ]
    return lax.ppermute(x, ("rows", "cols"), pairs)


def swap(x, axis, size, bit):
    return lax.ppermute(x, axis, [(i, i ^ bit) for i in range(size)])


def attention(rows, cols, queries, keys, values, positions):
    tokens = queries.shape[0]
    pos = positions.reshape(1, tokens)
    block = jax.ShapeDtypeStruct((1, 2 * tokens + POS_ROWS, HEAD_DIM), jnp.bfloat16)
    in_hbm = functools.partial(pltpu.with_memory_space_constraint, memory_space=pltpu.HBM)
    own, near_pos = call(
        pack_kernel,
        (
            block,
            jax.ShapeDtypeStruct((1, tokens), jnp.float32),
        ),
        [in_hbm(x) for x in (keys, values, pos)],
    )
    acc = jax.ShapeDtypeStruct((HEADS * tokens, 2 * HEAD_DIM), jnp.float32)
    qpos = jax.ShapeDtypeStruct((tokens, LANES), jnp.float32)
    heads = jax.ShapeDtypeStruct((HEADS * tokens, HEAD_DIM), jnp.bfloat16)

    def together(pieces, *groups):
        shapes = tuple(
            jax.ShapeDtypeStruct(
                (sum(pieces[i].shape[0] for i in g),) + pieces[0].shape[1:], jnp.bfloat16
            )
            for g in groups
        )
        return call(functools.partial(bundle_kernel, groups), shapes, pieces)

    def work(pieces):
        return 4 * HEADS * tokens * HEAD_DIM * tokens * sum(p.shape[0] for p in pieces)

    def further(before, pieces):
        return call(
            functools.partial(next_kernel, len(pieces)), acc,
            [qs, query_pos, before, *pieces], flops=work(pieces),
        )

    bit = rows // 2
    while bit >= 4:
        own = jnp.concatenate([own, swap(own, "rows", rows, bit)], axis=0)
        bit //= 2
    z2 = hop(own, rows, cols, 2, 0)
    z1 = hop(own, rows, cols, 1, 0)
    xo = hop(own, rows, cols, 0, 2)
    xz3 = hop(z2, rows, cols, 1, 2)
    (b12,) = together([z2, z1], (0, 1))
    zb = hop(b12, rows, cols, 0, 2)
    z3 = hop(z2, rows, cols, 1, 0)
    (b1,) = together([own, z2, z1, xo], (0, 1, 2, 3))
    cb1 = swap(b1, "cols", cols, 1)
    acc1, query_pos, qs = call(
        functools.partial(first_kernel, 1), (acc, qpos, heads), [queries, near_pos, b1], flops=work([b1])
    )
    cc = swap(xz3, "cols", cols, 1)
    acc2 = further(acc1, [cb1])
    cz3 = swap(z3, "cols", cols, 1)
    czb = swap(zb, "cols", cols, 1)
    acc3 = further(acc2, [zb, xz3, cc])
    acc4 = further(acc3, [z3, cz3])
    pieces = [czb, b1, cb1, xz3, cc, zb, z3, cz3]
    return call(
        functools.partial(last_kernel, 1),
        jax.ShapeDtypeStruct(queries.shape, jnp.bfloat16),
        [qs, query_pos, acc4, *pieces],
        scratch=[
            pltpu.VMEM(acc.shape, acc.dtype),
            pltpu.VMEM(queries.shape, jnp.bfloat16),
            pltpu.SemaphoreType.DMA((HEADS,)),
        ],
        flops=work([pieces[0]]), out_spec=pl.BlockSpec(memory_space=pltpu.HBM),
    )


def solution(mesh):
    rows, cols = mesh.shape["rows"], mesh.shape["cols"]

    def shards(*arrays):
        return attention(rows, cols, *arrays)

    return jax.shard_map(
        shards,
        mesh=mesh,
        in_specs=(
            P(("groups", "rows", "cols"), None),
            P(("groups", "rows", "cols"), None),
            P(("groups", "rows", "cols"), None),
            P(("groups", "rows", "cols")),
        ),
        out_specs=P(("groups", "rows", "cols"), None),
        check_vma=False,
    )
```

```python
import functools
import math

import jax
import jax.numpy as jnp
from jax import lax
from jax.experimental import pallas as pl
from jax.experimental.pallas import tpu as pltpu
from jax.sharding import PartitionSpec as P

HEADS = 8
HEAD_DIM = 128
LANES = 128
POS_ROWS = 16
HIGH_SHIFT = 7
LOW_MASK = 127

den_low = 1e-18
den_high = 1e37
neg_fill = -1e30
vmem_bytes = 16 * 1024 * 1024


VMEM = pl.BlockSpec(memory_space=pltpu.VMEM)


def call(kernel, out_shape, operands, scratch=(), flops=0, out_spec=VMEM):
    size = sum(x.size * x.dtype.itemsize for x in operands)
    return pl.pallas_call(
        kernel,
        out_shape=out_shape,
        in_specs=[VMEM] * len(operands),
        out_specs=jax.tree.map(lambda s: out_spec, out_shape),
        scratch_shapes=scratch,
        compiler_params=pltpu.CompilerParams(vmem_limit_bytes=vmem_bytes),
        cost_estimate=pl.CostEstimate(flops=flops, bytes_accessed=size, transcendentals=0),
    )(*operands)


def pack_kernel(key_ref, value_ref, pos_ref, block_ref, near_pos_ref):
    tokens = key_ref.shape[0]
    near_pos_ref[...] = pos_ref[...].astype(jnp.float32)
    block_ref[0, :tokens, :] = key_ref[...]
    block_ref[0, tokens : 2 * tokens, :] = value_ref[...]
    row = lax.broadcasted_iota(jnp.int32, (POS_ROWS, LANES), 0)
    tile = jnp.zeros((POS_ROWS, LANES), jnp.float32)
    for j in range(tokens // LANES):
        pos = pos_ref[:, j * LANES : (j + 1) * LANES]
        high = (pos >> HIGH_SHIFT).astype(jnp.float32)
        low = (pos & LOW_MASK).astype(jnp.float32)
        tile = jnp.where(row == 2 * j, jnp.broadcast_to(high, tile.shape), tile)
        tile = jnp.where(row == 2 * j + 1, jnp.broadcast_to(low, tile.shape), tile)
    block_ref[0, 2 * tokens :, :] = tile.astype(block_ref.dtype)


def block_rows(ref):
    return (ref.shape[1] - POS_ROWS) // 2


def keys_of(ref, i):
    return ref[i, : block_rows(ref), :]


def values_of(ref, i):
    rows = block_rows(ref)
    return jnp.concatenate(
        [ref[i, rows : 2 * rows, :], jnp.ones((rows, HEAD_DIM), jnp.bfloat16)], axis=1
    )


def visible_of(ref, i, query_pos):
    rows = block_rows(ref)
    parts = ref[i, 2 * rows :, :].astype(jnp.float32)
    return jnp.concatenate(
        [
            parts[2 * j : 2 * j + 1] * (LOW_MASK + 1) + parts[2 * j + 1 : 2 * j + 2] <= query_pos
            for j in range(rows // LANES)
        ],
        axis=1,
    )


def dot_keys(q, keys):
    return lax.dot_general(
        q, keys, (((1,), (1,)), ((), ())), preferred_element_type=jnp.float32
    )


def absorb(qs_ref, query_pos, total, blocks, at, stack, by_lane=False):
    pre = HEAD_DIM ** (-0.5) * math.log2(math.e)
    q = qs_ref[at, :]
    for j in range(0, len(blocks), 2):
        group = blocks[j : j + 2]
        scores = dot_keys(q, jnp.concatenate([keys_of(*b) for b in group], axis=0))
        mask = jnp.concatenate([visible_of(*b, query_pos) for b in group], axis=1)
        mask = jnp.concatenate([mask] * stack, axis=0)
        weights = jnp.where(mask, jnp.exp2(scores * pre), 0.0).astype(jnp.bfloat16)
        values = jnp.concatenate([values_of(*b) for b in group], axis=0)
        if by_lane:
            part = jnp.dot(weights, values[:, :HEAD_DIM], preferred_element_type=jnp.float32)
            wide = weights.astype(jnp.float32)
            sums = wide[:, :LANES]
            for j in range(LANES, wide.shape[1], LANES):
                sums = sums + wide[:, j : j + LANES]
            part = jnp.concatenate([part, sums], axis=1)
        else:
            part = jnp.dot(weights, values, preferred_element_type=jnp.float32)
        total = part if total is None else total + part
    return total


def accumulate(qs_ref, query_pos, before, after, pieces, groups=None, by_lane=False):
    stack = 4 if HEADS % 4 == 0 else 1
    tokens = query_pos.shape[0]
    span = stack * tokens
    small = sum(p.shape[0] for p in pieces) <= 8
    for r in groups or range(HEADS // stack):
        at = slice(r * span, (r + 1) * span)
        start = None if before is None else before[at, :]
        if small:
            blocks = [(p, i) for p in pieces for i in range(p.shape[0])]
            after[at, :] = absorb(qs_ref, query_pos, start, blocks, at, stack, by_lane)
            continue
        after[at, :] = jnp.zeros((span, 2 * HEAD_DIM), jnp.float32) if start is None else start
        for p in pieces:

            def pair(i, carry, p=p):
                blocks = [(p, 2 * i), (p, 2 * i + 1)]
                after[at, :] = absorb(qs_ref, query_pos, after[at, :], blocks, at, stack, by_lane)
                return carry

            lax.fori_loop(0, p.shape[0] // 2, pair, 0)


def bundle(pieces, out_ref):
    at = 0
    for p in pieces:
        out_ref[at : at + p.shape[0]] = p[...]
        at += p.shape[0]


def bundle_kernel(groups, *refs):
    for group, out_ref in zip(groups, refs[-len(groups) :]):
        bundle([refs[i] for i in group], out_ref)


def first_kernel(count, q_ref, pos_ref, *refs):
    acc_ref, qpos_ref, qs_ref = refs[count:]
    tokens = pos_ref.shape[1]
    for h in range(HEADS):
        qs_ref[h * tokens : (h + 1) * tokens, :] = q_ref[:, h * HEAD_DIM : (h + 1) * HEAD_DIM]
    qpos_ref[...] = jnp.transpose(
        jnp.broadcast_to(pos_ref[...], (LANES, tokens))
    )
    accumulate(qs_ref, qpos_ref[...], None, acc_ref, refs[:count], by_lane=True)


def next_kernel(count, spread, qs_ref, qpos_ref, before_ref, *refs):
    acc_ref = refs[count]
    accumulate(qs_ref, qpos_ref[...], before_ref, acc_ref, refs[:count], by_lane=True)
    if spread:
        sums = jnp.sum(acc_ref[:, HEAD_DIM:], axis=1, keepdims=True)
        acc_ref[:, HEAD_DIM:] = jnp.broadcast_to(sums, (sums.shape[0], HEAD_DIM))


def last_kernel(count, qs_ref, qpos_ref, before_ref, *refs):
    pieces = refs[:-4]
    o_ref, acc_ref, out_ref, sems = refs[-4:]
    query_pos = qpos_ref[...]
    tokens = query_pos.shape[0]
    scale = HEAD_DIM ** (-0.5)
    stack = 4 if HEADS % 4 == 0 else 1

    def copy(r):
        at = slice(r * stack * HEAD_DIM, (r + 1) * stack * HEAD_DIM)
        return pltpu.make_async_copy(out_ref.at[:, at], o_ref.at[:, at], sems.at[r])

    def divide(r):
        for h in range(r * stack, (r + 1) * stack):
            part = acc_ref[h * tokens : (h + 1) * tokens, :]
            out_ref[:, h * HEAD_DIM : (h + 1) * HEAD_DIM] = (
                part[:, :HEAD_DIM] / part[:, HEAD_DIM:]
            ).astype(out_ref.dtype)

    groups = range(HEADS // stack)
    for r in groups:
        accumulate(qs_ref, query_pos, before_ref, acc_ref, pieces[:count], (r,))
        divide(r)
        copy(r).start()
    den = acc_ref[:, HEAD_DIM:]
    good = (den >= den_low) & (den <= den_high)
    worst = jnp.min(jnp.where(good, 1.0, 0.0))
    for r in groups:
        copy(r).wait()

    @pl.when(worst < 0.5)
    def _():
        def one_head(h, carry):
            at = pl.ds(pl.multiple_of(h * tokens, tokens), tokens)
            q = qs_ref[at, :]
            top = jnp.full((tokens, 1), neg_fill, jnp.float32)
            for ref in pieces:

                def raise_top(i, top, ref=ref):
                    s = dot_keys(q, keys_of(ref, i)) * scale
                    s = jnp.where(visible_of(ref, i, query_pos), s, neg_fill)
                    return jnp.maximum(top, jnp.max(s, axis=1, keepdims=True))

                top = lax.fori_loop(0, ref.shape[0], raise_top, top)
            total = jnp.zeros((tokens, 2 * HEAD_DIM), jnp.float32)
            for ref in pieces:

                def add(i, total, ref=ref):
                    s = dot_keys(q, keys_of(ref, i)) * scale
                    w = jnp.where(visible_of(ref, i, query_pos), jnp.exp(s - top), 0.0)
                    return total + jnp.dot(
                        w.astype(jnp.bfloat16),
                        values_of(ref, i),
                        preferred_element_type=jnp.float32,
                    )

                total = lax.fori_loop(0, ref.shape[0], add, total)
            acc_ref[at, :] = total
            return carry

        lax.fori_loop(0, HEADS, one_head, 0)
        for r in groups:
            divide(r)
            copy(r).start()
        for r in groups:
            copy(r).wait()


def hop(x, rows, cols, row_bit, col_bit):
    pairs = [
        (r * cols + c, (r ^ row_bit) * cols + (c ^ col_bit)) for r in range(rows) for c in range(cols)
    ]
    return lax.ppermute(x, ("rows", "cols"), pairs)


def swap(x, axis, size, bit):
    return lax.ppermute(x, axis, [(i, i ^ bit) for i in range(size)])


def attention(rows, cols, queries, keys, values, positions):
    tokens = queries.shape[0]
    pos = positions.reshape(1, tokens)
    block = jax.ShapeDtypeStruct((1, 2 * tokens + POS_ROWS, HEAD_DIM), jnp.bfloat16)
    in_hbm = functools.partial(pltpu.with_memory_space_constraint, memory_space=pltpu.HBM)
    own, near_pos = call(
        pack_kernel,
        (
            block,
            jax.ShapeDtypeStruct((1, tokens), jnp.float32),
        ),
        [in_hbm(x) for x in (keys, values, pos)],
    )
    acc = jax.ShapeDtypeStruct((HEADS * tokens, 2 * HEAD_DIM), jnp.float32)
    qpos = jax.ShapeDtypeStruct((tokens, LANES), jnp.float32)
    heads = jax.ShapeDtypeStruct((HEADS * tokens, HEAD_DIM), jnp.bfloat16)

    def together(pieces, *groups):
        shapes = tuple(
            jax.ShapeDtypeStruct(
                (sum(pieces[i].shape[0] for i in g),) + pieces[0].shape[1:], jnp.bfloat16
            )
            for g in groups
        )
        return call(functools.partial(bundle_kernel, groups), shapes, pieces)

    def work(pieces):
        return 4 * HEADS * tokens * HEAD_DIM * tokens * sum(p.shape[0] for p in pieces)

    def further(before, pieces, spread=False):
        return call(
            functools.partial(next_kernel, len(pieces), spread), acc,
            [qs, query_pos, before, *pieces], flops=work(pieces),
        )

    bit = rows // 2
    while bit >= 4:
        own = jnp.concatenate([own, swap(own, "rows", rows, bit)], axis=0)
        bit //= 2
    z2 = hop(own, rows, cols, 2, 0)
    z1 = hop(own, rows, cols, 1, 0)
    xo = hop(own, rows, cols, 0, 2)
    xz3 = hop(z2, rows, cols, 1, 2)
    (b12,) = together([z2, z1], (0, 1))
    zb = hop(b12, rows, cols, 0, 2)
    z3 = hop(z2, rows, cols, 1, 0)
    (b1,) = together([own, z2, z1, xo], (0, 1, 2, 3))
    cb1 = swap(b1, "cols", cols, 1)
    acc1, query_pos, qs = call(
        functools.partial(first_kernel, 1), (acc, qpos, heads), [queries, near_pos, b1], flops=work([b1])
    )
    cc = swap(xz3, "cols", cols, 1)
    acc2 = further(acc1, [cb1])
    cz3 = swap(z3, "cols", cols, 1)
    czb = swap(zb, "cols", cols, 1)
    acc3 = further(acc2, [zb, xz3, cc])
    acc4 = further(acc3, [z3, cz3], True)
    pieces = [czb, b1, cb1, xz3, cc, zb, z3, cz3]
    return call(
        functools.partial(last_kernel, 1),
        jax.ShapeDtypeStruct(queries.shape, jnp.bfloat16),
        [qs, query_pos, acc4, *pieces],
        scratch=[
            pltpu.VMEM(acc.shape, acc.dtype),
            pltpu.VMEM(queries.shape, jnp.bfloat16),
            pltpu.SemaphoreType.DMA((HEADS,)),
        ],
        flops=work([pieces[0]]), out_spec=pl.BlockSpec(memory_space=pltpu.HBM),
    )


def solution(mesh):
    rows, cols = mesh.shape["rows"], mesh.shape["cols"]

    def shards(*arrays):
        return attention(rows, cols, *arrays)

    return jax.shard_map(
        shards,
        mesh=mesh,
        in_specs=(
            P(("groups", "rows", "cols"), None),
            P(("groups", "rows", "cols"), None),
            P(("groups", "rows", "cols"), None),
            P(("groups", "rows", "cols")),
        ),
        out_specs=P(("groups", "rows", "cols"), None),
        check_vma=False,
    )
```
